32 devices in a mesh: tm: 4 (over y, x), rows: 8 (over z, core).
Axes of the slice: x: 2, y: 2, z: 4, core: 2. Of those that a mesh axis runs over, the one named last changes fastest.
Arguments:
- latents: bfloat16 [4, 32, 104, 384], P('tm', 'rows')
- row_valid: int32 [32], P('rows'), may hold values from 0 to 1, as said below
- norm_gain: float32 [384], replicated, may hold values from 0.25 to 1.75
- conv_weight: bfloat16 [10368, 384], P('tm'), may hold values from -0.0625 to 0.0625
- attn_gain: float32 [384], replicated, may hold values from 0.25 to 1.75
- w_query: bfloat16 [384, 384], replicated
- w_key: bfloat16 [384, 384], replicated
- w_value: bfloat16 [384, 384], replicated, may hold values from -0.3125 to 0.3125
- w_out: bfloat16 [384, 384], replicated, may hold values from -0.3125 to 0.3125
- cotangent: bfloat16 [4, 32, 104, 384], P('tm', 'rows'), may hold values from -6 to 6
Outputs:
- input_grad: bfloat16 [4, 32, 104, 384], P('tm', 'rows')
- conv_weight_grad: float32 [10368, 384], P(('tm', 'rows'))
- attn_weight_grad: float32 [1536, 384], P(('tm', 'rows'))
The draws below stay inside these ranges and needn't reach their ends.
Inputs may be any that keep to these rules, and one draw needn't show every extreme that they name: row_valid is 1 on rows 0 to 15 and 0 on row 31; the rows between may be either.
All inputs are finite; a program needn't handle non-finite values.
Results may differ from the reference program's by a relative error of at most 0.01.
Values may be sent and summed in bfloat16 or wider, within the bound.
A program may use at most 192 MiB of HBM per device.

```python
import math
import jax
import jax.numpy as jnp
from jax import lax

C = 384
W = 104
R_DEV = 4
FRAMES = 4
H = 32
N_ROWS = 8


def draw_latents(key, part):
    full_shape = (FRAMES, H, W, C)
    return jnp.clip(jax.random.normal(key, full_shape, jnp.float32), -6.0, 6.0).astype(jnp.bfloat16)


def draw_row_valid(key, part):
    coin = jax.random.randint(jax.random.fold_in(key, 5), (H,), 0, 2)
    row_at = jnp.arange(H)
    picked = jnp.where(row_at < H // 2, 1, coin)
    return jnp.where(row_at == H - 1, 0, picked).astype(jnp.int32)


def query_key_pair(key):
    sub_one, sub_two = jax.random.split(jax.random.fold_in(key, 11), 2)
    root_scale = 1.0 / math.sqrt(C)
    base_draw = jnp.clip(jax.random.normal(sub_one, (C, C), jnp.float32), -5.0, 5.0) * root_scale
    other_draw = jnp.clip(jax.random.normal(sub_two, (C, C), jnp.float32), -5.0, 5.0) * root_scale
    query_draw = base_draw
    key_draw = other_draw
    return (query_draw, key_draw)


def draw_w_query(key, part):
    return query_key_pair(key)[0].astype(jnp.bfloat16)


def draw_w_key(key, part):
    return query_key_pair(key)[1].astype(jnp.bfloat16)


def shard_levels(rng, dims, shards, least, high):
    def one(axis_at, parts):
        heights = jax.random.uniform(jax.random.fold_in(jax.random.fold_in(rng, 6), axis_at), (parts,), jnp.float32, least / len(shards), high / len(shards))
        return jnp.repeat(jnp.exp(heights), dims[axis_at] // parts).reshape((-1,) + (1,) * (len(dims) - axis_at - 1))

    loudness = one(*shards[0])
    for cut in shards[1:]:
        loudness = loudness * one(*cut)
    return loudness


def gaussian(stream_key, dims, scale, bound, cuts=(), kind=jnp.bfloat16):
    result = scale * jax.random.normal(stream_key, dims, jnp.float32)
    if cuts:
        result = result * shard_levels(stream_key, dims, cuts, -0.22, 0.18)
    return jnp.clip(result, -bound, bound).astype(kind)


def setup_inputs(seed: int = 0) -> dict:
    splits = jax.random.split(jax.random.key(seed), 11)
    return {
        "latents": draw_latents(jax.random.fold_in(splits[10], 71), 0),
        "row_valid": draw_row_valid(jax.random.fold_in(splits[10], 71), 0),
        "norm_gain": jnp.clip(1.0 + 0.15 * jax.random.normal(splits[2], (C,), jnp.float32), 0.25, 1.75),
        "conv_weight": gaussian(splits[3], (27 * C, C), (27 * C) ** -0.5, 0.0625, ((0, 4),)),
        "attn_gain": jnp.clip(1.0 + 0.15 * jax.random.normal(splits[4], (C,), jnp.float32), 0.25, 1.75),
        "w_query": draw_w_query(jax.random.fold_in(splits[10], 71), 0),
        "w_key": draw_w_key(jax.random.fold_in(splits[10], 71), 0),
        "w_value": gaussian(splits[7], (C, C), C ** -0.5, 0.3125),
        "w_out": gaussian(splits[8], (C, C), C ** -0.5, 0.3125),
        "cotangent": gaussian(splits[9], (FRAMES, H, W, C), 1.0, 6.0, ((0, 4), (1, 8))),
    }


epsilon = 1e-06

def silu_slope(inputs):
    logistic = jax.nn.sigmoid(inputs)
    return logistic * (1.0 + inputs * (1.0 - logistic))

def rounded_terms(terms):
    return lax.optimization_barrier(terms.astype(jnp.bfloat16)).astype(jnp.float32)

def frame_backward(queries, keys_all, values_all, d_attended, key_flags):
    channels = queries.shape[1]
    inv_root = 1.0 / math.sqrt(channels)
    slab_size = R_DEV * W
    block_q = queries.reshape(N_ROWS, slab_size, channels)
    block_d = d_attended.reshape(N_ROWS, slab_size, channels)

    def one_slab(running, pair_in):
        slab_q, slab_d = pair_in
        scores = jnp.dot(slab_q, keys_all.T, preferred_element_type=jnp.float32) * inv_root
        scores = jnp.where(key_flags[None, :] > 0, scores, -jnp.inf)
        row_max = lax.optimization_barrier(jnp.max(scores, axis=1, keepdims=True))
        exponent = jnp.exp(scores - row_max)
        weights = exponent / lax.optimization_barrier(jnp.sum(exponent, axis=1, keepdims=True))
        weights_b = weights.astype(jnp.bfloat16)
        attended = jnp.dot(weights_b, values_all, preferred_element_type=jnp.float32).astype(jnp.bfloat16)
        d_weights = jnp.dot(slab_d, values_all.T, preferred_element_type=jnp.float32)
        row_delta = lax.optimization_barrier(jnp.sum(slab_d.astype(jnp.float32) * attended.astype(jnp.float32), axis=1, keepdims=True))
        d_scores = (weights * (d_weights - row_delta) * inv_root).astype(jnp.bfloat16)
        d_query = jnp.dot(d_scores, keys_all, preferred_element_type=jnp.float32).astype(jnp.bfloat16)
        key_term = rounded_terms(jnp.dot(d_scores.T, slab_q, preferred_element_type=jnp.float32))
        value_term = rounded_terms(jnp.dot(weights_b.T, slab_d, preferred_element_type=jnp.float32))
        return ((running[0] + key_term, running[1] + value_term), (attended, d_query))
    start_sums = (jnp.zeros(keys_all.shape, jnp.float32), jnp.zeros(values_all.shape, jnp.float32))
    key_value, per_slab = lax.scan(one_slab, start_sums, (block_q, block_d))
    attended = per_slab[0].reshape(-1, channels)
    d_query = per_slab[1].reshape(-1, channels)
    return (attended, d_query, key_value[0].astype(jnp.bfloat16), key_value[1].astype(jnp.bfloat16))

def reference(latents, row_valid, norm_gain, conv_weight, attn_gain, w_query, w_key, w_value, w_out, cotangent):
    frame_count, height, col_count, channels = latents.shape
    frame_cells = height * col_count
    cell_total = frame_count * frame_cells
    grad_scale = 1.0 / math.sqrt(cell_total)
    cell_factor = jnp.broadcast_to(row_valid.astype(jnp.float32)[None, :, None], (frame_count, height, col_count)).reshape(cell_total, 1)
    inputs = latents.reshape(cell_total, channels).astype(jnp.float32)
    first_scale = lax.rsqrt(lax.optimization_barrier(jnp.mean(inputs * inputs, axis=1, keepdims=True)) + epsilon)
    normed_one = inputs * first_scale
    gated_in = normed_one * norm_gain
    conv_in = (jax.nn.silu(gated_in) * cell_factor).astype(jnp.bfloat16).reshape(frame_count, height, col_count, channels)
    history = jnp.pad(conv_in, ((2, 0), (1, 1), (1, 1), (0, 0)))
    conv_out = jnp.zeros((cell_total, channels), jnp.float32)
    for time_tap in range(3):
        for row_tap in range(3):
            for col_tap in range(3):
                tap_index = 9 * time_tap + 3 * row_tap + col_tap
                tap_rows = history[time_tap:time_tap + frame_count, row_tap:row_tap + height, col_tap:col_tap + col_count].reshape(cell_total, channels)
                conv_out = conv_out + jnp.dot(tap_rows, conv_weight[tap_index * channels:(tap_index + 1) * channels], preferred_element_type=jnp.float32)
    mixed_out = (inputs + conv_out).astype(jnp.bfloat16)
    mixed_f = mixed_out.astype(jnp.float32)
    second_scale = lax.rsqrt(lax.optimization_barrier(jnp.mean(mixed_f * mixed_f, axis=1, keepdims=True)) + epsilon)
    normed_two = mixed_f * second_scale
    attn_in = (normed_two * attn_gain).astype(jnp.bfloat16)
    queries = jnp.dot(attn_in, w_query, preferred_element_type=jnp.float32).astype(jnp.bfloat16)
    keys_own = jnp.dot(attn_in, w_key, preferred_element_type=jnp.float32).astype(jnp.bfloat16)
    values_own = jnp.dot(attn_in, w_value, preferred_element_type=jnp.float32).astype(jnp.bfloat16)
    live_cells = cell_factor > 0
    grad_out = jnp.where(live_cells, cotangent.reshape(cell_total, channels), jnp.zeros((), jnp.bfloat16))
    d_attended = jnp.dot(grad_out, w_out.T, preferred_element_type=jnp.float32).astype(jnp.bfloat16)
    key_flags = jnp.repeat(row_valid.astype(jnp.bfloat16), col_count)

    def per_frame(frame_in):
        frame_q, frame_k, frame_v, frame_d = frame_in
        return frame_backward(frame_q, frame_k, frame_v, frame_d, key_flags)
    framed = (queries.reshape(frame_count, frame_cells, channels), keys_own.reshape(frame_count, frame_cells, channels), values_own.reshape(frame_count, frame_cells, channels), d_attended.reshape(frame_count, frame_cells, channels))
    attended, d_query, d_key, d_value = lax.map(per_frame, framed)
    attended = attended.reshape(cell_total, channels)
    d_query = d_query.reshape(cell_total, channels)
    d_key = d_key.reshape(cell_total, channels)
    d_value = d_value.reshape(cell_total, channels)
    attn_weight_grad = jnp.concatenate([jnp.dot(attn_in.T, d_query, preferred_element_type=jnp.float32), jnp.dot(attn_in.T, d_key, preferred_element_type=jnp.float32), jnp.dot(attn_in.T, d_value, preferred_element_type=jnp.float32), jnp.dot(attended.T, grad_out, preferred_element_type=jnp.float32)], axis=0) * grad_scale
    d_normed = jnp.dot(d_query, w_query.T, preferred_element_type=jnp.float32) + jnp.dot(d_key, w_key.T, preferred_element_type=jnp.float32) + jnp.dot(d_value, w_value.T, preferred_element_type=jnp.float32)
    scaled_two = attn_gain * d_normed
    d_mixed = grad_out.astype(jnp.float32) + second_scale * (scaled_two - normed_two * lax.optimization_barrier(jnp.mean(scaled_two * normed_two, axis=1, keepdims=True)))
    d_conv = d_mixed.astype(jnp.bfloat16)
    spread_block = jnp.pad(d_conv.reshape(frame_count, height, col_count, channels), ((0, 2), (1, 1), (1, 1), (0, 0)))
    d_input = jnp.zeros((cell_total, channels), jnp.float32)
    grad_blocks = []
    for time_tap in range(3):
        for row_tap in range(3):
            for col_tap in range(3):
                tap_index = 9 * time_tap + 3 * row_tap + col_tap
                tap_rows = history[time_tap:time_tap + frame_count, row_tap:row_tap + height, col_tap:col_tap + col_count].reshape(cell_total, channels)
                grad_blocks.append(jnp.dot(tap_rows.T, d_conv, preferred_element_type=jnp.float32) * grad_scale)
                ahead_rows = spread_block[2 - time_tap:2 - time_tap + frame_count, 2 - row_tap:2 - row_tap + height, 2 - col_tap:2 - col_tap + col_count].reshape(cell_total, channels)
                d_input = d_input + jnp.dot(ahead_rows, conv_weight[tap_index * channels:(tap_index + 1) * channels].T, preferred_element_type=jnp.float32)
    conv_weight_grad = jnp.concatenate(grad_blocks, axis=0)
    d_input = d_input * cell_factor
    scaled_one = norm_gain * d_input * silu_slope(gated_in)
    input_grad = d_mixed + first_scale * (scaled_one - normed_one * lax.optimization_barrier(jnp.mean(scaled_one * normed_one, axis=1, keepdims=True)))
    return (input_grad.astype(jnp.bfloat16).reshape(latents.shape), conv_weight_grad, attn_weight_grad)
```

```python
import functools
import math

import jax
import jax.numpy as jnp
from jax import lax
from jax.experimental import pallas as pl
from jax.experimental.pallas import tpu as pltpu
from jax.sharding import PartitionSpec as P

epsilon = 1e-06
MESH = pl.DeviceIdType.MESH
ANY = pl.BlockSpec(memory_space=pl.ANY)
IN_VMEM = pl.BlockSpec(memory_space=pltpu.VMEM)
FLAG_ROWS = 16


def contract_last(first_op, second_op):
    return lax.dot_general(
        first_op, second_op, (((1,), (1,)), ((), ())), preferred_element_type=jnp.float32
    )


def contract_first(first_op, second_op):
    return lax.dot_general(
        first_op, second_op, (((0,), (0,)), ((), ())), preferred_element_type=jnp.float32
    )


def dot(first_op, second_op):
    return jnp.dot(first_op, second_op, preferred_element_type=jnp.float32)


def silu_slope(inputs):
    logistic = jax.nn.sigmoid(inputs)
    return logistic * (1.0 + inputs * (1.0 - logistic))


def params(collective_id):
    return pltpu.CompilerParams(
        collective_id=collective_id, has_side_effects=True, vmem_limit_bytes=40 * 1024 * 1024
    )


def signal(barrier, tm_at, row_at):
    pl.semaphore_signal(barrier, inc=1, device_id=(tm_at, row_at), device_id_type=MESH)


def remote(src, dst, send_sem, recv_sem, tm_at, row_at):
    return pltpu.make_async_remote_copy(
        src_ref=src,
        dst_ref=dst,
        send_sem=send_sem,
        recv_sem=recv_sem,
        device_id=(tm_at, row_at),
        device_id_type=MESH,
    )


def slabs_kernel(frames, slabs, x, o, local_sem, send_sem, recv_sem):
    t, r = lax.axis_index("tm"), lax.axis_index("rows")
    rows = x.shape[0]
    has_above, has_below = r > 0, r < slabs - 1
    others = [lax.rem(t + d, frames) for d in range(frames)]
    barrier = pltpu.get_barrier_semaphore()
    for d in range(1, frames):
        signal(barrier, others[d], r)

    @pl.when(has_above)
    def _():
        for d in range(frames):
            signal(barrier, others[d], r - 1)

    @pl.when(has_below)
    def _():
        for d in range(frames):
            signal(barrier, others[d], r + 1)

    sides = has_above.astype(jnp.int32) + has_below.astype(jnp.int32)
    pl.semaphore_wait(barrier, frames - 1 + frames * sides)

    own = pltpu.make_async_copy(x, o.at[t, pl.ds(1, rows)], local_sem)
    own.start()
    slab = [
        remote(x, o.at[t, pl.ds(1, rows)], send_sem.at[d], recv_sem.at[d], others[d], r)
        for d in range(1, frames)
    ]
    down = [
        remote(
            x.at[rows - 1],
            o.at[t, 0],
            send_sem.at[frames + d],
            recv_sem.at[frames + d],
            others[d],
            r + 1,
        )
        for d in range(frames)
    ]
    up = [
        remote(
            x.at[0],
            o.at[t, rows + 1],
            send_sem.at[2 * frames + d],
            recv_sem.at[2 * frames + d],
            others[d],
            r - 1,
        )
        for d in range(frames)
    ]

    @pl.when(has_below)
    def _():
        for copy in down:
            copy.start()

    @pl.when(has_above)
    def _():
        for copy in up:
            copy.start()

    for copy in slab:
        copy.start()
    own.wait()
    for copy in slab:
        copy.wait()

    @pl.when(has_below)
    def _():
        for copy in down:
            copy.wait_send()
        for copy in up:
            copy.wait_recv()

    @pl.when(has_above)
    def _():
        for copy in up:
            copy.wait_send()
        for copy in down:
            copy.wait_recv()


def gather_slabs(block, collective_id):
    frames, slabs = lax.axis_size("tm"), lax.axis_size("rows")
    rows, cols, channels = block.shape
    result = pl.pallas_call(
        functools.partial(slabs_kernel, frames, slabs),
        out_shape=jax.ShapeDtypeStruct((frames, rows + 2, cols, channels), block.dtype),
        in_specs=[ANY],
        out_specs=ANY,
        scratch_shapes=[
            pltpu.SemaphoreType.DMA,
            pltpu.SemaphoreType.DMA((3 * frames,)),
            pltpu.SemaphoreType.DMA((3 * frames,)),
        ],
        compiler_params=params(collective_id),
    )(block)
    r = lax.axis_index("rows")
    row_at = lax.broadcasted_iota(jnp.int32, (1, rows + 2, 1, 1), 1)
    inside = ((row_at > 0) | (r > 0)) & ((row_at < rows + 1) | (r < slabs - 1))
    return jnp.where(inside, result, jnp.zeros((), block.dtype))


def swap_kernel(frames, count, *refs):
    xs, os = refs[:count], refs[count : 2 * count]
    local_sem, send_sem, recv_sem = refs[2 * count :]
    t, r = lax.axis_index("tm"), lax.axis_index("rows")
    others = [lax.rem(t + d, frames) for d in range(frames)]
    barrier = pltpu.get_barrier_semaphore()
    for d in range(1, frames):
        signal(barrier, others[d], r)
    pl.semaphore_wait(barrier, frames - 1)
    copies = []
    for i, (x, o) in enumerate(zip(xs, os)):
        for d in range(1, frames):
            copies.append(
                remote(
                    x.at[others[d]], o.at[t], send_sem.at[i, d], recv_sem.at[i, d], others[d], r
                )
            )
        copies.append(pltpu.make_async_copy(x.at[t], o.at[t], local_sem.at[i]))
    for copy in copies:
        copy.start()
    for copy in copies:
        copy.wait()


def swap_over_tm(arrays, collective_id):
    frames, count = lax.axis_size("tm"), len(arrays)
    return pl.pallas_call(
        functools.partial(swap_kernel, frames, count),
        out_shape=[jax.ShapeDtypeStruct(a.shape, a.dtype) for a in arrays],
        in_specs=[ANY] * count,
        out_specs=[ANY] * count,
        scratch_shapes=[
            pltpu.SemaphoreType.DMA((count,)),
            pltpu.SemaphoreType.DMA((count, frames)),
            pltpu.SemaphoreType.DMA((count, frames)),
        ],
        compiler_params=params(collective_id),
    )(*arrays)


def line_kernel(pairs, x, o, local_sem, send_sem, recv_sem):
    t, r = lax.axis_index("tm"), lax.axis_index("rows")
    q, c = lax.div(r, 2), lax.rem(r, 2)
    sibling = 2 * q + 1 - c
    has_left, has_right = q > 0, q < pairs - 1
    barrier = pltpu.get_barrier_semaphore()
    signal(barrier, t, sibling)

    @pl.when(has_left)
    def _():
        signal(barrier, t, r - 2)

    @pl.when(has_right)
    def _():
        signal(barrier, t, r + 2)

    pl.semaphore_wait(barrier, 1 + has_left.astype(jnp.int32) + has_right.astype(jnp.int32))

    own = pltpu.make_async_copy(x, o.at[r], local_sem)
    own.start()
    to_sibling = remote(x, o.at[r], send_sem.at[0, 0], recv_sem.at[0, 0], t, sibling)

    def held(step, side):
        return r - side * 2 * step

    def hop(step, side):
        at = held(step - 1, side)
        return remote(
            x if step == 1 else o.at[at],
            o.at[at],
            send_sem.at[1 if side > 0 else 2, step],
            recv_sem.at[1 if side > 0 else 2, step],
            t,
            r + 2 * side,
        )

    def hand(step, side):
        at = held(step, side)
        return remote(
            o.at[at],
            o.at[at],
            send_sem.at[3 if side > 0 else 4, step],
            recv_sem.at[3 if side > 0 else 4, step],
            t,
            sibling,
        )

    def arrives(step, side):
        return q - step >= 0 if side > 0 else q + step < pairs

    def sends(step, side):
        onward = has_right if side > 0 else has_left
        return onward if step == 1 else jnp.logical_and(onward, arrives(step - 1, side))

    for side in (1, -1):

        @pl.when(sends(1, side))
        def _():
            hop(1, side).start()

    to_sibling.start()
    for step in range(1, pairs):
        for side in (1, -1):

            @pl.when(arrives(step, side))
            def _():
                hop(step, side).wait_recv()

            if step < pairs - 1:

                @pl.when(sends(step + 1, side))
                def _():
                    hop(step + 1, side).start()

            @pl.when(arrives(step, side))
            def _():
                hand(step, side).start()

    own.wait()
    to_sibling.wait()
    for step in range(1, pairs):
        for side in (1, -1):

            @pl.when(sends(step, side))
            def _():
                hop(step, side).wait_send()

            @pl.when(arrives(step, side))
            def _():
                hand(step, side).wait()


def gather_rows(block, collective_id):
    slabs = lax.axis_size("rows")
    pairs = slabs // 2
    return pl.pallas_call(
        functools.partial(line_kernel, pairs),
        out_shape=jax.ShapeDtypeStruct((slabs,) + block.shape, block.dtype),
        in_specs=[ANY],
        out_specs=ANY,
        scratch_shapes=[
            pltpu.SemaphoreType.DMA,
            pltpu.SemaphoreType.DMA((5, pairs)),
            pltpu.SemaphoreType.DMA((5, pairs)),
        ],
        compiler_params=params(collective_id),
    )(block)


def sum_kernel(pairs, count, *refs):
    gs, os = refs[:count], refs[count : 2 * count]
    near, ready, far = (refs[(2 + i) * count : (3 + i) * count] for i in range(3))
    send_sem, recv_sem, far_send, far_recv = refs[5 * count :]
    t, r = lax.axis_index("tm"), lax.axis_index("rows")
    q, c = lax.div(r, 2), lax.rem(r, 2)
    sibling = 2 * q + 1 - c
    pair_at = [lax.rem(q + d, pairs) for d in range(pairs)]
    barrier = pltpu.get_barrier_semaphore()
    signal(barrier, t, sibling)
    for d in range(1, pairs):
        signal(barrier, t, 2 * pair_at[d] + c)
    pl.semaphore_wait(barrier, pairs)
    order = list(range(1, pairs)) + [0]
    near_copies, far_copies = {}, {}
    for d in order:
        for i in range(count):
            copy = remote(
                gs[i].at[2 * pair_at[d] + 1 - c],
                near[i].at[d],
                send_sem.at[i, d],
                recv_sem.at[i, d],
                t,
                sibling,
            )
            copy.start()
            near_copies[i, d] = copy
    for d in order:
        for i in range(count):
            near_copies[i, d].wait_recv()
            total = gs[i][2 * pair_at[d] + c].astype(jnp.float32) + near[i][d].astype(jnp.float32)
            if d == 0:
                os[i][...] = total
            else:
                ready[i][d] = total.astype(jnp.bfloat16)
                copy = remote(
                    ready[i].at[d],
                    far[i].at[d],
                    far_send.at[i, d],
                    far_recv.at[i, d],
                    t,
                    2 * pair_at[d] + c,
                )
                copy.start()
                far_copies[i, d] = copy
    for d in range(1, pairs):
        for i in range(count):
            far_copies[i, d].wait_recv()
            os[i][...] += far[i][d].astype(jnp.float32)
    for copy in list(near_copies.values()) + list(far_copies.values()):
        copy.wait_send()


def sum_over_rows(arrays, collective_id):
    slabs, count = lax.axis_size("rows"), len(arrays)
    pairs = slabs // 2
    slots = [pltpu.VMEM((pairs,) + a.shape[1:], jnp.bfloat16) for a in arrays]
    return pl.pallas_call(
        functools.partial(sum_kernel, pairs, count),
        out_shape=[jax.ShapeDtypeStruct(a.shape[1:], jnp.float32) for a in arrays],
        in_specs=[IN_VMEM] * count,
        out_specs=[IN_VMEM] * count,
        scratch_shapes=slots * 3 + [pltpu.SemaphoreType.DMA((count, pairs))] * 4,
        compiler_params=params(collective_id),
    )(*arrays)


def gather_taps(frames_block, tap_at, frames, rows_dev):
    cols, channels = frames_block.shape[2:]
    wide = jnp.pad(frames_block, ((0, 0), (0, 0), (1, 1), (0, 0)))
    shifted = jnp.stack([wide[:, :, s : s + cols] for s in range(3)])
    taps = [
        lax.dynamic_slice(
            shifted, (col_at, frame_at, row_at, 0, 0), (1, frames, rows_dev, cols, channels)
        ).reshape(frames * rows_dev * cols, channels)
        for frame_at, row_at, col_at in tap_at
    ]
    return jnp.concatenate(taps, axis=1)


def per_device(
    latents, row_valid, norm_gain, conv_weight, attn_gain, w_query, w_key, w_value, w_out, cotangent
):
    bf16 = jnp.bfloat16
    shape_all = latents.shape
    rows_dev, col_count, channels = shape_all[1:]
    slab_size = rows_dev * col_count
    frames, slabs = lax.axis_size("tm"), lax.axis_size("rows")
    t = lax.axis_index("tm")
    grad_scale = 1.0 / math.sqrt(frames * slabs * slab_size)
    inv_root = 1.0 / math.sqrt(channels)

    own_rows = conv_weight.shape[0]
    tap_total = own_rows * frames // channels
    tap_count = max(
        -(-((i * own_rows) % channels + own_rows) // channels) for i in range(frames)
    )
    first_tap = lax.div(t * own_rows, channels)
    weight_from = t * own_rows - first_tap * channels
    own_weight = lax.dynamic_update_slice(
        jnp.zeros((tap_count * channels, channels), bf16), conv_weight, (weight_from, 0)
    )
    taps = []
    for j in range(tap_count):
        k = jnp.minimum(first_tap + j, tap_total - 1)
        taps.append((lax.div(k, 9), lax.div(lax.rem(k, 9), 3), lax.rem(k, 3)))

    cell_factor = jnp.repeat(row_valid.astype(jnp.float32), col_count)[:, None]
    live_cells = cell_factor > 0
    inputs = latents.reshape(slab_size, channels).astype(jnp.float32)
    first_scale = lax.rsqrt(jnp.mean(inputs * inputs, axis=1, keepdims=True) + epsilon)
    normed_one = inputs * first_scale
    gated_in = normed_one * norm_gain
    conv_in = (jax.nn.silu(gated_in) * cell_factor).astype(bf16)

    grad_out = jnp.where(live_cells, cotangent.reshape(slab_size, channels), jnp.zeros((), bf16))

    history = gather_slabs(conv_in.reshape(rows_dev, col_count, channels), 0)
    history = jnp.pad(history, ((2, 0), (0, 0), (0, 0), (0, 0)))
    columns = gather_taps(history, taps, frames, rows_dev)
    conv_terms = dot(columns, own_weight).astype(bf16).reshape(frames, slab_size, channels)
    (conv_terms,) = swap_over_tm([conv_terms], 1)
    conv_out = jnp.sum(conv_terms.astype(jnp.float32), axis=0)

    mixed_f = (inputs + conv_out).astype(bf16).astype(jnp.float32)
    second_scale = lax.rsqrt(jnp.mean(mixed_f * mixed_f, axis=1, keepdims=True) + epsilon)
    normed_two = mixed_f * second_scale
    attn_in = (normed_two * attn_gain).astype(bf16)

    flag_rows = jnp.pad(row_valid.astype(bf16), (0, FLAG_ROWS - rows_dev))
    flag_rows = jnp.broadcast_to(flag_rows[:, None], (FLAG_ROWS, channels))
    block_size = slab_size + FLAG_ROWS
    gathered = gather_rows(jnp.concatenate([attn_in, flag_rows], axis=0), 2)
    flags_all = jnp.repeat(gathered[:, slab_size : slab_size + rows_dev, 0], col_count, axis=1)
    flags_all = jnp.pad(flags_all, ((0, 0), (0, FLAG_ROWS))).reshape(1, slabs * block_size)
    cells = gathered.reshape(slabs * block_size, channels)

    queries = dot(attn_in, w_query).astype(bf16)
    key_side = contract_last(queries, w_key).astype(bf16)
    d_attended = contract_last(grad_out, w_out).astype(bf16)
    value_side = contract_last(d_attended, w_value).astype(bf16)

    scores = contract_last(key_side, cells) * inv_root
    scores = jnp.where(flags_all > 0, scores, -jnp.inf)
    row_max = jnp.max(scores, axis=1, keepdims=True)
    exponent = jnp.exp(scores - row_max)
    row_total = jnp.sum(exponent, axis=1, keepdims=True)
    weights = exponent / row_total
    weights_b = weights.astype(bf16)
    weighted = dot(weights_b, cells)
    weighted_b = weighted.astype(bf16)
    attended = dot(weighted_b, w_value).astype(bf16)
    d_weights = contract_last(value_side, cells)
    row_delta = jnp.sum(value_side.astype(jnp.float32) * weighted, axis=1, keepdims=True)
    d_scores = (weights * (d_weights - row_delta) * inv_root).astype(bf16)
    d_cells = dot(d_scores, cells).astype(bf16)
    d_query = dot(d_cells, w_key).astype(bf16)
    key_terms = contract_first(
        jnp.concatenate([d_scores, weights_b], axis=0),
        jnp.concatenate([key_side, value_side], axis=0),
    ).astype(bf16)
    grad_stack = (
        jnp.concatenate(
            [
                contract_first(attn_in, d_query),
                contract_first(d_cells, queries),
                contract_first(weighted_b, d_attended),
                contract_first(attended, grad_out),
            ],
            axis=0,
        )
        * grad_scale
    ).astype(bf16)
    stack_rows = grad_stack.shape[0] // (frames * slabs)
    grad_stack = (
        grad_stack.reshape(frames, slabs, stack_rows, channels)
        .transpose(1, 0, 2, 3)
        .reshape(slabs, frames * stack_rows, channels)
    )
    d_attn_in, grad_stack = sum_over_rows(
        [key_terms.reshape(slabs, block_size, channels), grad_stack], 3
    )
    d_normed = contract_last(d_query, w_query) + d_attn_in[:slab_size]
    scaled_two = attn_gain * d_normed
    d_mixed = grad_out.astype(jnp.float32) + second_scale * (
        scaled_two - normed_two * jnp.mean(scaled_two * normed_two, axis=1, keepdims=True)
    )
    d_conv = d_mixed.astype(bf16)

    spread = gather_slabs(d_conv.reshape(rows_dev, col_count, channels), 4)
    d_conv_all = spread[:, 1 : 1 + rows_dev].reshape(frames * slab_size, channels)
    spread = jnp.pad(spread, ((0, 2), (0, 0), (0, 0), (0, 0)))
    back_columns = gather_taps(
        spread, [(2 - a, 2 - b, 2 - c) for a, b, c in taps], frames, rows_dev
    )
    back_weight = (
        own_weight.reshape(tap_count, channels, channels)
        .transpose(1, 0, 2)
        .reshape(channels, tap_count * channels)
    )
    input_terms = contract_last(back_columns, back_weight).astype(bf16)
    input_terms, stack_terms = swap_over_tm(
        [
            input_terms.reshape(frames, slab_size, channels),
            grad_stack.astype(bf16).reshape(frames, stack_rows, channels),
        ],
        5,
    )
    attn_weight_grad = jnp.sum(stack_terms.astype(jnp.float32), axis=0)

    weight_terms = (contract_first(columns, d_conv_all) * grad_scale).astype(bf16)
    weight_terms = lax.dynamic_slice(weight_terms, (weight_from, 0), (own_rows, channels))
    (conv_weight_grad,) = sum_over_rows([weight_terms.reshape(slabs, -1, channels)], 6)

    d_input = jnp.sum(input_terms.astype(jnp.float32), axis=0) * cell_factor
    scaled_one = norm_gain * d_input * silu_slope(gated_in)
    input_grad = d_mixed + first_scale * (
        scaled_one - normed_one * jnp.mean(scaled_one * normed_one, axis=1, keepdims=True)
    )
    return (input_grad.astype(bf16).reshape(shape_all), conv_weight_grad, attn_weight_grad)


def solution(mesh):
    return jax.shard_map(
        per_device,
        mesh=mesh,
        in_specs=(
            P("tm", "rows", None, None),
            P("rows"),
            P(),
            P("tm", None),
            P(),
            P(),
            P(),
            P(),
            P(),
            P("tm", "rows", None, None),
        ),
        out_specs=(P("tm", "rows", None, None), P(("tm", "rows"), None), P(("tm", "rows"), None)),
        check_vma=False,
    )
```

```python
import functools
import math

import jax
import jax.numpy as jnp
from jax import lax
from jax.experimental import pallas as pl
from jax.experimental.pallas import tpu as pltpu
from jax.sharding import PartitionSpec as P

epsilon = 1e-06
MESH = pl.DeviceIdType.MESH
ANY = pl.BlockSpec(memory_space=pl.ANY)
IN_VMEM = pl.BlockSpec(memory_space=pltpu.VMEM)
FLAG_ROWS = 16


def contract_last(first_op, second_op):
    return lax.dot_general(
        first_op, second_op, (((1,), (1,)), ((), ())), preferred_element_type=jnp.float32
    )


def contract_first(first_op, second_op):
    return lax.dot_general(
        first_op, second_op, (((0,), (0,)), ((), ())), preferred_element_type=jnp.float32
    )


def dot(first_op, second_op):
    return jnp.dot(first_op, second_op, preferred_element_type=jnp.float32)


def silu_slope(inputs):
    logistic = jax.nn.sigmoid(inputs)
    return logistic * (1.0 + inputs * (1.0 - logistic))


def params(collective_id):
    return pltpu.CompilerParams(
        collective_id=collective_id, has_side_effects=True, vmem_limit_bytes=40 * 1024 * 1024
    )


def signal(barrier, tm_at, row_at):
    pl.semaphore_signal(barrier, inc=1, device_id=(tm_at, row_at), device_id_type=MESH)


def remote(src, dst, send_sem, recv_sem, tm_at, row_at):
    return pltpu.make_async_remote_copy(
        src_ref=src,
        dst_ref=dst,
        send_sem=send_sem,
        recv_sem=recv_sem,
        device_id=(tm_at, row_at),
        device_id_type=MESH,
    )


def slabs_kernel(frames, slabs, x, o, local_sem, send_sem, recv_sem):
    t, r = lax.axis_index("tm"), lax.axis_index("rows")
    rows = x.shape[0]
    has_above, has_below = r > 0, r < slabs - 1
    others = [lax.rem(t + d, frames) for d in range(frames)]
    barrier = pltpu.get_barrier_semaphore()
    for d in range(1, frames):
        signal(barrier, others[d], r)

    @pl.when(has_above)
    def _():
        for d in range(frames):
            signal(barrier, others[d], r - 1)

    @pl.when(has_below)
    def _():
        for d in range(frames):
            signal(barrier, others[d], r + 1)

    sides = has_above.astype(jnp.int32) + has_below.astype(jnp.int32)
    pl.semaphore_wait(barrier, frames - 1 + frames * sides)

    own = pltpu.make_async_copy(x, o.at[t, pl.ds(1, rows)], local_sem)
    own.start()
    slab = [
        remote(x, o.at[t, pl.ds(1, rows)], send_sem.at[d], recv_sem.at[d], others[d], r)
        for d in range(1, frames)
    ]
    down = [
        remote(
            x.at[rows - 1],
            o.at[t, 0],
            send_sem.at[frames + d],
            recv_sem.at[frames + d],
            others[d],
            r + 1,
        )
        for d in range(frames)
    ]
    up = [
        remote(
            x.at[0],
            o.at[t, rows + 1],
            send_sem.at[2 * frames + d],
            recv_sem.at[2 * frames + d],
            others[d],
            r - 1,
        )
        for d in range(frames)
    ]

    @pl.when(has_below)
    def _():
        for copy in down:
            copy.start()

    @pl.when(has_above)
    def _():
        for copy in up:
            copy.start()

    for copy in slab:
        copy.start()
    own.wait()
    for copy in slab:
        copy.wait()

    @pl.when(has_below)
    def _():
        for copy in down:
            copy.wait_send()
        for copy in up:
            copy.wait_recv()

    @pl.when(has_above)
    def _():
        for copy in up:
            copy.wait_send()
        for copy in down:
            copy.wait_recv()


def gather_slabs(block, collective_id):
    frames, slabs = lax.axis_size("tm"), lax.axis_size("rows")
    rows, cols, channels = block.shape
    result = pl.pallas_call(
        functools.partial(slabs_kernel, frames, slabs),
        out_shape=jax.ShapeDtypeStruct((frames, rows + 2, cols, channels), block.dtype),
        in_specs=[ANY],
        out_specs=ANY,
        scratch_shapes=[
            pltpu.SemaphoreType.DMA,
            pltpu.SemaphoreType.DMA((3 * frames,)),
            pltpu.SemaphoreType.DMA((3 * frames,)),
        ],
        compiler_params=params(collective_id),
    )(block)
    r = lax.axis_index("rows")
    row_at = lax.broadcasted_iota(jnp.int32, (1, rows + 2, 1, 1), 1)
    inside = ((row_at > 0) | (r > 0)) & ((row_at < rows + 1) | (r < slabs - 1))
    return jnp.where(inside, result, jnp.zeros((), block.dtype))


def swap_kernel(frames, count, *refs):
    xs, os = refs[:count], refs[count : 2 * count]
    local_sem, send_sem, recv_sem = refs[2 * count :]
    t, r = lax.axis_index("tm"), lax.axis_index("rows")
    others = [lax.rem(t + d, frames) for d in range(frames)]
    barrier = pltpu.get_barrier_semaphore()
    for d in range(1, frames):
        signal(barrier, others[d], r)
    pl.semaphore_wait(barrier, frames - 1)
    copies = []
    for i, (x, o) in enumerate(zip(xs, os)):
        for d in range(1, frames):
            copies.append(
                remote(
                    x.at[others[d]], o.at[t], send_sem.at[i, d], recv_sem.at[i, d], others[d], r
                )
            )
        copies.append(pltpu.make_async_copy(x.at[t], o.at[t], local_sem.at[i]))
    for copy in copies:
        copy.start()
    for copy in copies:
        copy.wait()


def swap_over_tm(arrays, collective_id):
    frames, count = lax.axis_size("tm"), len(arrays)
    return pl.pallas_call(
        functools.partial(swap_kernel, frames, count),
        out_shape=[jax.ShapeDtypeStruct(a.shape, a.dtype) for a in arrays],
        in_specs=[ANY] * count,
        out_specs=[ANY] * count,
        scratch_shapes=[
            pltpu.SemaphoreType.DMA((count,)),
            pltpu.SemaphoreType.DMA((count, frames)),
            pltpu.SemaphoreType.DMA((count, frames)),
        ],
        compiler_params=params(collective_id),
    )(*arrays)


def line_kernel(pairs, x, o, local_sem, send_sem, recv_sem):
    t, r = lax.axis_index("tm"), lax.axis_index("rows")
    q, c = lax.div(r, 2), lax.rem(r, 2)
    sibling = 2 * q + 1 - c
    has_left, has_right = q > 0, q < pairs - 1
    barrier = pltpu.get_barrier_semaphore()
    signal(barrier, t, sibling)

    @pl.when(has_left)
    def _():
        signal(barrier, t, r - 2)

    @pl.when(has_right)
    def _():
        signal(barrier, t, r + 2)

    pl.semaphore_wait(barrier, 1 + has_left.astype(jnp.int32) + has_right.astype(jnp.int32))

    own = pltpu.make_async_copy(x, o.at[r], local_sem)
    own.start()
    to_sibling = remote(x, o.at[r], send_sem.at[0, 0], recv_sem.at[0, 0], t, sibling)

    def held(step, side):
        return r - side * 2 * step

    def hop(step, side):
        at = held(step - 1, side)
        return remote(
            x if step == 1 else o.at[at],
            o.at[at],
            send_sem.at[1 if side > 0 else 2, step],
            recv_sem.at[1 if side > 0 else 2, step],
            t,
            r + 2 * side,
        )

    def hand(step, side):
        at = held(step, side)
        return remote(
            o.at[at],
            o.at[at],
            send_sem.at[3 if side > 0 else 4, step],
            recv_sem.at[3 if side > 0 else 4, step],
            t,
            sibling,
        )

    def arrives(step, side):
        return q - step >= 0 if side > 0 else q + step < pairs

    def sends(step, side):
        onward = has_right if side > 0 else has_left
        return onward if step == 1 else jnp.logical_and(onward, arrives(step - 1, side))

    for side in (1, -1):

        @pl.when(sends(1, side))
        def _():
            hop(1, side).start()

    to_sibling.start()
    for step in range(1, pairs):
        for side in (1, -1):

            @pl.when(arrives(step, side))
            def _():
                hop(step, side).wait_recv()

            if step < pairs - 1:

                @pl.when(sends(step + 1, side))
                def _():
                    hop(step + 1, side).start()

            @pl.when(arrives(step, side))
            def _():
                hand(step, side).start()

    own.wait()
    to_sibling.wait()
    for step in range(1, pairs):
        for side in (1, -1):

            @pl.when(sends(step, side))
            def _():
                hop(step, side).wait_send()

            @pl.when(arrives(step, side))
            def _():
                hand(step, side).wait()


def gather_rows(block, collective_id):
    slabs = lax.axis_size("rows")
    pairs = slabs // 2
    return pl.pallas_call(
        functools.partial(line_kernel, pairs),
        out_shape=jax.ShapeDtypeStruct((slabs,) + block.shape, block.dtype),
        in_specs=[ANY],
        out_specs=ANY,
        scratch_shapes=[
            pltpu.SemaphoreType.DMA,
            pltpu.SemaphoreType.DMA((5, pairs)),
            pltpu.SemaphoreType.DMA((5, pairs)),
        ],
        compiler_params=params(collective_id),
    )(block)


def sum_kernel(pairs, count, *refs):
    gs, os = refs[:count], refs[count : 2 * count]
    near, ready, far = (refs[(2 + i) * count : (3 + i) * count] for i in range(3))
    send_sem, recv_sem, far_send, far_recv = refs[5 * count :]
    t, r = lax.axis_index("tm"), lax.axis_index("rows")
    q, c = lax.div(r, 2), lax.rem(r, 2)
    sibling = 2 * q + 1 - c
    pair_at = [lax.rem(q + d, pairs) for d in range(pairs)]
    barrier = pltpu.get_barrier_semaphore()
    signal(barrier, t, sibling)
    for d in range(1, pairs):
        signal(barrier, t, 2 * pair_at[d] + c)
    pl.semaphore_wait(barrier, pairs)
    order = list(range(1, pairs)) + [0]
    near_copies, far_copies = {}, {}
    for d in order:
        for i in range(count):
            copy = remote(
                gs[i].at[2 * pair_at[d] + 1 - c],
                near[i].at[d],
                send_sem.at[i, d],
                recv_sem.at[i, d],
                t,
                sibling,
            )
            copy.start()
            near_copies[i, d] = copy
    for d in order:
        for i in range(count):
            near_copies[i, d].wait_recv()
            total = gs[i][2 * pair_at[d] + c].astype(jnp.float32) + near[i][d].astype(jnp.float32)
            if d == 0:
                os[i][...] = total
            else:
                ready[i][d] = total.astype(jnp.bfloat16)
                copy = remote(
                    ready[i].at[d],
                    far[i].at[d],
                    far_send.at[i, d],
                    far_recv.at[i, d],
                    t,
                    2 * pair_at[d] + c,
                )
                copy.start()
                far_copies[i, d] = copy
    for d in range(1, pairs):
        for i in range(count):
            far_copies[i, d].wait_recv()
            os[i][...] += far[i][d].astype(jnp.float32)
    for copy in list(near_copies.values()) + list(far_copies.values()):
        copy.wait_send()


def sum_over_rows(arrays, collective_id):
    slabs, count = lax.axis_size("rows"), len(arrays)
    pairs = slabs // 2
    slots = [pltpu.VMEM((pairs,) + a.shape[1:], jnp.bfloat16) for a in arrays]
    return pl.pallas_call(
        functools.partial(sum_kernel, pairs, count),
        out_shape=[jax.ShapeDtypeStruct(a.shape[1:], jnp.float32) for a in arrays],
        in_specs=[IN_VMEM] * count,
        out_specs=[IN_VMEM] * count,
        scratch_shapes=slots * 3 + [pltpu.SemaphoreType.DMA((count, pairs))] * 4,
        compiler_params=params(collective_id),
    )(*arrays)


def column_shifts(slabs, before, after):
    cols = slabs.shape[2]
    width = -(-cols // 16) * 16
    spare = width - cols
    edges = ((before, after), (0, 0))
    return jnp.stack(
        [jnp.pad(slabs, edges + ((1, spare - 1), (0, 0)))]
        + [jnp.pad(slabs, edges + ((0, spare), (0, 0)))]
        + [jnp.pad(slabs[:, :, 1:], edges + ((0, spare + 1), (0, 0)))]
    )


def taps_kernel(rows, cols, transposed, taps, shifted, weight, out, columns):
    f = pl.program_id(0)
    width, channels = shifted.shape[3:]
    count = taps.shape[0]
    total = None
    for j in range(count):
        window = shifted[taps[j, 2], taps[j, 0] + f, pl.ds(taps[j, 1], rows)]
        window = window.reshape(rows * width, channels)
        columns[:, j * channels : (j + 1) * channels] = window
        if transposed:
            term = contract_last(window, weight[j * channels : (j + 1) * channels, :])
            total = term if total is None else total + term
    if not transposed:
        total = dot(columns[...], weight[...])
    total = total.astype(out.dtype).reshape(rows, width, channels)
    out[0] = total[:, :cols]


def sum_taps(shifted, taps, weight, rows, cols, transposed):
    frames = shifted.shape[1] - 2
    width, channels = shifted.shape[3:]
    count = taps.shape[0]
    out = jax.ShapeDtypeStruct((frames, rows, cols, channels), jnp.bfloat16)
    out_spec = pl.BlockSpec((1, rows, cols, channels), lambda f: (f, 0, 0, 0))
    block = (rows * width, count * channels)
    columns = jax.ShapeDtypeStruct((frames * block[0], block[1]), jnp.bfloat16)
    columns_spec = pl.BlockSpec(block, lambda f: (f, 0))
    flops = 2 * frames * block[0] * block[1] * channels
    return pl.pallas_call(
        functools.partial(taps_kernel, rows, cols, transposed),
        grid=(frames,),
        out_shape=out if transposed else (out, columns),
        in_specs=[pl.BlockSpec(memory_space=pltpu.SMEM), IN_VMEM, IN_VMEM],
        out_specs=out_spec if transposed else (out_spec, columns_spec),
        scratch_shapes=[pltpu.VMEM(block, jnp.bfloat16)] if transposed else [],
        cost_estimate=pl.CostEstimate(flops=flops, bytes_accessed=20_000_000, transcendentals=0),
        compiler_params=pltpu.CompilerParams(vmem_limit_bytes=48 * 1024 * 1024),
    )(taps, shifted, weight)


def per_device(
    latents, row_valid, norm_gain, conv_weight, attn_gain, w_query, w_key, w_value, w_out, cotangent
):
    bf16 = jnp.bfloat16
    shape_all = latents.shape
    rows_dev, col_count, channels = shape_all[1:]
    slab_size = rows_dev * col_count
    frames, slabs = lax.axis_size("tm"), lax.axis_size("rows")
    t = lax.axis_index("tm")
    grad_scale = 1.0 / math.sqrt(frames * slabs * slab_size)
    inv_root = 1.0 / math.sqrt(channels)

    own_rows = conv_weight.shape[0]
    tap_total = own_rows * frames // channels
    tap_count = max(
        -(-((i * own_rows) % channels + own_rows) // channels) for i in range(frames)
    )
    first_tap = lax.div(t * own_rows, channels)
    weight_from = t * own_rows - first_tap * channels
    own_weight = lax.dynamic_update_slice(
        jnp.zeros((tap_count * channels, channels), bf16), conv_weight, (weight_from, 0)
    )
    k = jnp.minimum(first_tap + jnp.arange(tap_count, dtype=jnp.int32), tap_total - 1)
    taps = jnp.stack([k // 9, k % 9 // 3, k % 3], axis=1)

    cell_factor = jnp.repeat(row_valid.astype(jnp.float32), col_count)[:, None]
    live_cells = cell_factor > 0
    inputs = latents.reshape(slab_size, channels).astype(jnp.float32)
    first_scale = lax.rsqrt(jnp.mean(inputs * inputs, axis=1, keepdims=True) + epsilon)
    normed_one = inputs * first_scale
    gated_in = normed_one * norm_gain
    conv_in = (jax.nn.silu(gated_in) * cell_factor).astype(bf16)

    grad_out = jnp.where(live_cells, cotangent.reshape(slab_size, channels), jnp.zeros((), bf16))

    history = gather_slabs(conv_in.reshape(rows_dev, col_count, channels), 0)
    conv_terms, columns = sum_taps(
        column_shifts(history, 2, 0), taps, own_weight, rows_dev, col_count, False
    )
    conv_terms = conv_terms.reshape(frames, slab_size, channels)
    (conv_terms,) = swap_over_tm([conv_terms], 1)
    conv_out = jnp.sum(conv_terms.astype(jnp.float32), axis=0)

    mixed_f = (inputs + conv_out).astype(bf16).astype(jnp.float32)
    second_scale = lax.rsqrt(jnp.mean(mixed_f * mixed_f, axis=1, keepdims=True) + epsilon)
    normed_two = mixed_f * second_scale
    attn_in = (normed_two * attn_gain).astype(bf16)

    flag_rows = jnp.pad(row_valid.astype(bf16), (0, FLAG_ROWS - rows_dev))
    flag_rows = jnp.broadcast_to(flag_rows[:, None], (FLAG_ROWS, channels))
    block_size = slab_size + FLAG_ROWS
    gathered = gather_rows(jnp.concatenate([attn_in, flag_rows], axis=0), 2)
    flags_all = jnp.repeat(gathered[:, slab_size : slab_size + rows_dev, 0], col_count, axis=1)
    flags_all = jnp.pad(flags_all, ((0, 0), (0, FLAG_ROWS))).reshape(1, slabs * block_size)
    cells = gathered.reshape(slabs * block_size, channels)

    queries = dot(attn_in, w_query).astype(bf16)
    key_side = contract_last(queries, w_key).astype(bf16)
    d_attended = contract_last(grad_out, w_out).astype(bf16)
    value_side = contract_last(d_attended, w_value).astype(bf16)

    scores = contract_last(key_side, cells) * inv_root
    scores = jnp.where(flags_all > 0, scores, -jnp.inf)
    row_max = jnp.max(scores, axis=1, keepdims=True)
    exponent = jnp.exp(scores - row_max)
    row_total = jnp.sum(exponent, axis=1, keepdims=True)
    weights = exponent / row_total
    weights_b = weights.astype(bf16)
    weighted = dot(weights_b, cells)
    weighted_b = weighted.astype(bf16)
    attended = dot(weighted_b, w_value).astype(bf16)
    d_weights = contract_last(value_side, cells)
    row_delta = jnp.sum(value_side.astype(jnp.float32) * weighted, axis=1, keepdims=True)
    d_scores = (weights * (d_weights - row_delta) * inv_root).astype(bf16)
    d_cells = dot(d_scores, cells).astype(bf16)
    d_query = dot(d_cells, w_key).astype(bf16)
    key_terms = contract_first(
        jnp.concatenate([d_scores, weights_b], axis=0),
        jnp.concatenate([key_side, value_side], axis=0),
    ).astype(bf16)
    grad_stack = (
        jnp.concatenate(
            [
                contract_first(attn_in, d_query),
                contract_first(d_cells, queries),
                contract_first(weighted_b, d_attended),
                contract_first(attended, grad_out),
            ],
            axis=0,
        )
        * grad_scale
    ).astype(bf16)
    stack_rows = grad_stack.shape[0] // (frames * slabs)
    grad_stack = (
        grad_stack.reshape(frames, slabs, stack_rows, channels)
        .transpose(1, 0, 2, 3)
        .reshape(slabs * frames * stack_rows, channels)
    )
    stack_terms = lax.psum_scatter(grad_stack, "rows", scatter_dimension=0, tiled=True)
    (d_attn_in,) = sum_over_rows([key_terms.reshape(slabs, block_size, channels)], 3)
    d_normed = contract_last(d_query, w_query) + d_attn_in[:slab_size]
    scaled_two = attn_gain * d_normed
    d_mixed = grad_out.astype(jnp.float32) + second_scale * (
        scaled_two - normed_two * jnp.mean(scaled_two * normed_two, axis=1, keepdims=True)
    )
    d_conv = d_mixed.astype(bf16)

    spread = gather_slabs(d_conv.reshape(rows_dev, col_count, channels), 4)
    spare = columns.shape[0] // (frames * rows_dev) - col_count
    d_conv_all = jnp.pad(spread[:, 1 : 1 + rows_dev], ((0, 0), (0, 0), (0, spare), (0, 0)))
    weight_terms = contract_first(columns, d_conv_all.reshape(-1, channels)) * grad_scale
    weight_terms = lax.dynamic_slice(
        weight_terms.astype(bf16), (weight_from, 0), (own_rows, channels)
    )
    block_rows = own_rows // slabs
    padded_rows = -(-block_rows // 16) * 16
    weight_terms = jnp.pad(
        weight_terms.reshape(slabs, block_rows, channels),
        ((0, 0), (0, padded_rows - block_rows), (0, 0)),
    )
    weight_sums = lax.psum_scatter(
        weight_terms.reshape(slabs * padded_rows, channels), "rows", scatter_dimension=0, tiled=True
    )
    conv_weight_grad = weight_sums[:block_rows].astype(jnp.float32)

    input_terms = sum_taps(
        column_shifts(spread, 0, 2), 2 - taps, own_weight, rows_dev, col_count, True
    )
    input_terms, stack_terms = swap_over_tm(
        [
            input_terms.reshape(frames, slab_size, channels),
            stack_terms.reshape(frames, stack_rows, channels),
        ],
        5,
    )
    attn_weight_grad = jnp.sum(stack_terms.astype(jnp.float32), axis=0)

    d_input = jnp.sum(input_terms.astype(jnp.float32), axis=0) * cell_factor
    scaled_one = norm_gain * d_input * silu_slope(gated_in)
    input_grad = d_mixed + first_scale * (
        scaled_one - normed_one * jnp.mean(scaled_one * normed_one, axis=1, keepdims=True)
    )
    return (input_grad.astype(bf16).reshape(shape_all), conv_weight_grad, attn_weight_grad)


def solution(mesh):
    return jax.shard_map(
        per_device,
        mesh=mesh,
        in_specs=(
            P("tm", "rows", None, None),
            P("rows"),
            P(),
            P("tm", None),
            P(),
            P(),
            P(),
            P(),
            P(),
            P("tm", "rows", None, None),
        ),
        out_specs=(P("tm", "rows", None, None), P(("tm", "rows"), None), P(("tm", "rows"), None)),
        check_vma=False,
    )
```

```python
import functools
import math

import jax
import jax.numpy as jnp
from jax import lax
from jax.experimental import pallas as pl
from jax.experimental.pallas import tpu as pltpu
from jax.sharding import PartitionSpec as P

epsilon = 1e-06
MESH = pl.DeviceIdType.MESH
ANY = pl.BlockSpec(memory_space=pl.ANY)
IN_VMEM = pl.BlockSpec(memory_space=pltpu.VMEM)
FLAG_ROWS = 16


def contract_last(first_op, second_op):
    return lax.dot_general(
        first_op, second_op, (((1,), (1,)), ((), ())), preferred_element_type=jnp.float32
    )


def contract_first(first_op, second_op):
    return lax.dot_general(
        first_op, second_op, (((0,), (0,)), ((), ())), preferred_element_type=jnp.float32
    )


def dot(first_op, second_op):
    return jnp.dot(first_op, second_op, preferred_element_type=jnp.float32)


def silu_slope(inputs):
    logistic = jax.nn.sigmoid(inputs)
    return logistic * (1.0 + inputs * (1.0 - logistic))


def params(collective_id):
    return pltpu.CompilerParams(
        collective_id=collective_id, has_side_effects=True, vmem_limit_bytes=40 * 1024 * 1024
    )


def signal(barrier, tm_at, row_at):
    pl.semaphore_signal(barrier, inc=1, device_id=(tm_at, row_at), device_id_type=MESH)


def remote(src, dst, send_sem, recv_sem, tm_at, row_at):
    return pltpu.make_async_remote_copy(
        src_ref=src,
        dst_ref=dst,
        send_sem=send_sem,
        recv_sem=recv_sem,
        device_id=(tm_at, row_at),
        device_id_type=MESH,
    )


def slabs_kernel(frames, slabs, x, o, local_sem, send_sem, recv_sem):
    t, r = lax.axis_index("tm"), lax.axis_index("rows")
    rows = x.shape[0]
    has_above, has_below = r > 0, r < slabs - 1
    others = [lax.rem(t + d, frames) for d in range(frames)]
    barrier = pltpu.get_barrier_semaphore()
    for d in range(1, frames):
        signal(barrier, others[d], r)

    @pl.when(has_above)
    def _():
        for d in range(frames):
            signal(barrier, others[d], r - 1)

    @pl.when(has_below)
    def _():
        for d in range(frames):
            signal(barrier, others[d], r + 1)

    sides = has_above.astype(jnp.int32) + has_below.astype(jnp.int32)
    pl.semaphore_wait(barrier, frames - 1 + frames * sides)

    own = pltpu.make_async_copy(x, o.at[t, pl.ds(1, rows)], local_sem)
    own.start()
    slab = [
        remote(x, o.at[t, pl.ds(1, rows)], send_sem.at[d], recv_sem.at[d], others[d], r)
        for d in range(1, frames)
    ]
    down = [
        remote(
            x.at[rows - 1],
            o.at[t, 0],
            send_sem.at[frames + d],
            recv_sem.at[frames + d],
            others[d],
            r + 1,
        )
        for d in range(frames)
    ]
    up = [
        remote(
            x.at[0],
            o.at[t, rows + 1],
            send_sem.at[2 * frames + d],
            recv_sem.at[2 * frames + d],
            others[d],
            r - 1,
        )
        for d in range(frames)
    ]

    @pl.when(has_below)
    def _():
        for copy in down:
            copy.start()

    @pl.when(has_above)
    def _():
        for copy in up:
            copy.start()

    for copy in slab:
        copy.start()
    own.wait()
    for copy in slab:
        copy.wait()

    @pl.when(has_below)
    def _():
        for copy in down:
            copy.wait_send()
        for copy in up:
            copy.wait_recv()

    @pl.when(has_above)
    def _():
        for copy in up:
            copy.wait_send()
        for copy in down:
            copy.wait_recv()


def gather_slabs(block, collective_id):
    frames, slabs = lax.axis_size("tm"), lax.axis_size("rows")
    rows, cols, channels = block.shape
    result = pl.pallas_call(
        functools.partial(slabs_kernel, frames, slabs),
        out_shape=jax.ShapeDtypeStruct((frames, rows + 2, cols, channels), block.dtype),
        in_specs=[ANY],
        out_specs=ANY,
        scratch_shapes=[
            pltpu.SemaphoreType.DMA,
            pltpu.SemaphoreType.DMA((3 * frames,)),
            pltpu.SemaphoreType.DMA((3 * frames,)),
        ],
        compiler_params=params(collective_id),
    )(block)
    r = lax.axis_index("rows")
    row_at = lax.broadcasted_iota(jnp.int32, (1, rows + 2, 1, 1), 1)
    inside = ((row_at > 0) | (r > 0)) & ((row_at < rows + 1) | (r < slabs - 1))
    return jnp.where(inside, result, jnp.zeros((), block.dtype))


def swap_kernel(frames, count, *refs):
    xs, os = refs[:count], refs[count : 2 * count]
    local_sem, send_sem, recv_sem = refs[2 * count :]
    t, r = lax.axis_index("tm"), lax.axis_index("rows")
    others = [lax.rem(t + d, frames) for d in range(frames)]
    barrier = pltpu.get_barrier_semaphore()
    for d in range(1, frames):
        signal(barrier, others[d], r)
    pl.semaphore_wait(barrier, frames - 1)
    copies = []
    for i, (x, o) in enumerate(zip(xs, os)):
        for d in range(1, frames):
            copies.append(
                remote(
                    x.at[others[d]], o.at[t], send_sem.at[i, d], recv_sem.at[i, d], others[d], r
                )
            )
        copies.append(pltpu.make_async_copy(x.at[t], o.at[t], local_sem.at[i]))
    for copy in copies:
        copy.start()
    for copy in copies:
        copy.wait()


def swap_over_tm(arrays, collective_id):
    frames, count = lax.axis_size("tm"), len(arrays)
    return pl.pallas_call(
        functools.partial(swap_kernel, frames, count),
        out_shape=[jax.ShapeDtypeStruct(a.shape, a.dtype) for a in arrays],
        in_specs=[ANY] * count,
        out_specs=[ANY] * count,
        scratch_shapes=[
            pltpu.SemaphoreType.DMA((count,)),
            pltpu.SemaphoreType.DMA((count, frames)),
            pltpu.SemaphoreType.DMA((count, frames)),
        ],
        compiler_params=params(collective_id),
    )(*arrays)


def line_kernel(pairs, x, o, local_sem, send_sem, recv_sem):
    t, r = lax.axis_index("tm"), lax.axis_index("rows")
    q, c = lax.div(r, 2), lax.rem(r, 2)
    sibling = 2 * q + 1 - c
    has_left, has_right = q > 0, q < pairs - 1
    barrier = pltpu.get_barrier_semaphore()
    signal(barrier, t, sibling)

    @pl.when(has_left)
    def _():
        signal(barrier, t, r - 2)

    @pl.when(has_right)
    def _():
        signal(barrier, t, r + 2)

    pl.semaphore_wait(barrier, 1 + has_left.astype(jnp.int32) + has_right.astype(jnp.int32))

    own = pltpu.make_async_copy(x, o.at[r], local_sem)
    own.start()
    to_sibling = remote(x, o.at[r], send_sem.at[0, 0], recv_sem.at[0, 0], t, sibling)

    def held(step, side):
        return r - side * 2 * step

    def hop(step, side):
        at = held(step - 1, side)
        return remote(
            x if step == 1 else o.at[at],
            o.at[at],
            send_sem.at[1 if side > 0 else 2, step],
            recv_sem.at[1 if side > 0 else 2, step],
            t,
            r + 2 * side,
        )

    def hand(step, side):
        at = held(step, side)
        return remote(
            o.at[at],
            o.at[at],
            send_sem.at[3 if side > 0 else 4, step],
            recv_sem.at[3 if side > 0 else 4, step],
            t,
            sibling,
        )

    def arrives(step, side):
        return q - step >= 0 if side > 0 else q + step < pairs

    def sends(step, side):
        onward = has_right if side > 0 else has_left
        return onward if step == 1 else jnp.logical_and(onward, arrives(step - 1, side))

    for side in (1, -1):

        @pl.when(sends(1, side))
        def _():
            hop(1, side).start()

    to_sibling.start()
    for step in range(1, pairs):
        for side in (1, -1):

            @pl.when(arrives(step, side))
            def _():
                hop(step, side).wait_recv()

            if step < pairs - 1:

                @pl.when(sends(step + 1, side))
                def _():
                    hop(step + 1, side).start()

            @pl.when(arrives(step, side))
            def _():
                hand(step, side).start()

    own.wait()
    to_sibling.wait()
    for step in range(1, pairs):
        for side in (1, -1):

            @pl.when(sends(step, side))
            def _():
                hop(step, side).wait_send()

            @pl.when(arrives(step, side))
            def _():
                hand(step, side).wait()


def gather_rows(block, collective_id):
    slabs = lax.axis_size("rows")
    pairs = slabs // 2
    return pl.pallas_call(
        functools.partial(line_kernel, pairs),
        out_shape=jax.ShapeDtypeStruct((slabs,) + block.shape, block.dtype),
        in_specs=[ANY],
        out_specs=ANY,
        scratch_shapes=[
            pltpu.SemaphoreType.DMA,
            pltpu.SemaphoreType.DMA((5, pairs)),
            pltpu.SemaphoreType.DMA((5, pairs)),
        ],
        compiler_params=params(collective_id),
    )(block)


def sum_kernel(pairs, count, *refs):
    gs, os = refs[:count], refs[count : 2 * count]
    near, ready, far = (refs[(2 + i) * count : (3 + i) * count] for i in range(3))
    send_sem, recv_sem, far_send, far_recv = refs[5 * count :]
    t, r = lax.axis_index("tm"), lax.axis_index("rows")
    q, c = lax.div(r, 2), lax.rem(r, 2)
    sibling = 2 * q + 1 - c
    pair_at = [lax.rem(q + d, pairs) for d in range(pairs)]
    barrier = pltpu.get_barrier_semaphore()
    signal(barrier, t, sibling)
    for d in range(1, pairs):
        signal(barrier, t, 2 * pair_at[d] + c)
    pl.semaphore_wait(barrier, pairs)
    order = list(range(1, pairs)) + [0]
    near_copies, far_copies = {}, {}
    for d in order:
        for i in range(count):
            copy = remote(
                gs[i].at[2 * pair_at[d] + 1 - c],
                near[i].at[d],
                send_sem.at[i, d],
                recv_sem.at[i, d],
                t,
                sibling,
            )
            copy.start()
            near_copies[i, d] = copy
    for d in order:
        for i in range(count):
            near_copies[i, d].wait_recv()
            total = gs[i][2 * pair_at[d] + c].astype(jnp.float32) + near[i][d].astype(jnp.float32)
            if d == 0:
                os[i][...] = total
            else:
                ready[i][d] = total.astype(jnp.bfloat16)
                copy = remote(
                    ready[i].at[d],
                    far[i].at[d],
                    far_send.at[i, d],
                    far_recv.at[i, d],
                    t,
                    2 * pair_at[d] + c,
                )
                copy.start()
                far_copies[i, d] = copy
    for d in range(1, pairs):
        for i in range(count):
            far_copies[i, d].wait_recv()
            os[i][...] += far[i][d].astype(jnp.float32)
    for copy in list(near_copies.values()) + list(far_copies.values()):
        copy.wait_send()


def sum_over_rows(arrays, collective_id):
    slabs, count = lax.axis_size("rows"), len(arrays)
    pairs = slabs // 2
    slots = [pltpu.VMEM((pairs,) + a.shape[1:], jnp.bfloat16) for a in arrays]
    return pl.pallas_call(
        functools.partial(sum_kernel, pairs, count),
        out_shape=[jax.ShapeDtypeStruct(a.shape[1:], jnp.float32) for a in arrays],
        in_specs=[IN_VMEM] * count,
        out_specs=[IN_VMEM] * count,
        scratch_shapes=slots * 3 + [pltpu.SemaphoreType.DMA((count, pairs))] * 4,
        compiler_params=params(collective_id),
    )(*arrays)


def column_shifts(slabs, before, after):
    cols = slabs.shape[2]
    width = -(-cols // 16) * 16
    spare = width - cols
    edges = ((before, after), (0, 0))
    return jnp.stack(
        [jnp.pad(slabs, edges + ((1, spare - 1), (0, 0)))]
        + [jnp.pad(slabs, edges + ((0, spare), (0, 0)))]
        + [jnp.pad(slabs[:, :, 1:], edges + ((0, spare + 1), (0, 0)))]
    )


def taps_kernel(rows, cols, transposed, taps, shifted, weight, out, columns):
    f = pl.program_id(0)
    width, channels = shifted.shape[3:]
    count = taps.shape[0]
    total = None
    for j in range(count):
        window = shifted[taps[j, 2], taps[j, 0] + f, pl.ds(taps[j, 1], rows)]
        window = window.reshape(rows * width, channels)
        columns[:, j * channels : (j + 1) * channels] = window
        if transposed:
            term = contract_last(window, weight[j * channels : (j + 1) * channels, :])
            total = term if total is None else total + term
    if not transposed:
        total = dot(columns[...], weight[...])
    total = total.astype(out.dtype).reshape(rows, width, channels)
    out[0] = total[:, :cols]


def sum_taps(shifted, taps, weight, rows, cols, transposed):
    frames = shifted.shape[1] - 2
    width, channels = shifted.shape[3:]
    count = taps.shape[0]
    out = jax.ShapeDtypeStruct((frames, rows, cols, channels), jnp.bfloat16)
    out_spec = pl.BlockSpec((1, rows, cols, channels), lambda f: (f, 0, 0, 0))
    block = (rows * width, count * channels)
    columns = jax.ShapeDtypeStruct((frames * block[0], block[1]), jnp.bfloat16)
    columns_spec = pl.BlockSpec(block, lambda f: (f, 0))
    flops = 2 * frames * block[0] * block[1] * channels
    return pl.pallas_call(
        functools.partial(taps_kernel, rows, cols, transposed),
        grid=(frames,),
        out_shape=out if transposed else (out, columns),
        in_specs=[pl.BlockSpec(memory_space=pltpu.SMEM), IN_VMEM, IN_VMEM],
        out_specs=out_spec if transposed else (out_spec, columns_spec),
        scratch_shapes=[pltpu.VMEM(block, jnp.bfloat16)] if transposed else [],
        cost_estimate=pl.CostEstimate(flops=flops, bytes_accessed=20_000_000, transcendentals=0),
        compiler_params=pltpu.CompilerParams(vmem_limit_bytes=48 * 1024 * 1024),
    )(taps, shifted, weight)


def attention_kernel(
    inv_root, cells, bias, key_side, value_side, weighted_out, d_cells_out, terms, exponents, total
):
    slabs = cells.shape[0]
    rows, channels = key_side.shape

    def score(n, row_max):
        scores = contract_last(key_side[...], cells[n]) * inv_root + bias[n]
        exponents[n] = scores
        return jnp.maximum(row_max, jnp.max(scores, axis=1, keepdims=True))

    row_max = lax.fori_loop(0, slabs, score, jnp.full((rows, 1), -jnp.inf, jnp.float32))
    total[...] = jnp.zeros_like(total)

    def weigh(n, row_total):
        exponent = jnp.exp(exponents[n] - row_max)
        exponents[n] = exponent
        total[...] += dot(exponent.astype(jnp.bfloat16), cells[n])
        return row_total + jnp.sum(exponent, axis=1, keepdims=True)

    row_total = lax.fori_loop(0, slabs, weigh, jnp.zeros((rows, 1), jnp.float32))
    inverse = 1.0 / row_total
    weighted = total[...] * inverse
    weighted_out[...] = weighted.astype(jnp.bfloat16)
    row_delta = jnp.sum(value_side[...].astype(jnp.float32) * weighted, axis=1, keepdims=True)
    total[...] = jnp.zeros_like(total)

    def back(n, carry):
        d_weights = contract_last(value_side[...], cells[n])
        weights = exponents[n] * inverse
        d_scores = (weights * (d_weights - row_delta) * inv_root).astype(jnp.bfloat16)
        total[...] += dot(d_scores, cells[n])
        slab_terms = contract_first(d_scores, key_side[...])
        slab_terms += contract_first(weights.astype(jnp.bfloat16), value_side[...])
        terms[n] = slab_terms.astype(jnp.bfloat16)
        return carry

    lax.fori_loop(0, slabs, back, 0)
    d_cells_out[...] = total[...].astype(jnp.bfloat16)


def attention(cells, bias, key_side, value_side):
    slabs, block_size, channels = cells.shape
    rows = key_side.shape[0]
    side = jax.ShapeDtypeStruct((rows, channels), jnp.bfloat16)
    work = rows * slabs * block_size
    return pl.pallas_call(
        functools.partial(attention_kernel, 1.0 / math.sqrt(channels)),
        out_shape=(side, side, jax.ShapeDtypeStruct(cells.shape, jnp.bfloat16)),
        in_specs=[IN_VMEM] * 4,
        out_specs=(IN_VMEM,) * 3,
        scratch_shapes=[
            pltpu.VMEM((slabs, rows, block_size), jnp.float32),
            pltpu.VMEM((rows, channels), jnp.float32),
        ],
        cost_estimate=pl.CostEstimate(
            flops=12 * work * channels, bytes_accessed=8_000_000, transcendentals=work
        ),
        compiler_params=pltpu.CompilerParams(vmem_limit_bytes=48 * 1024 * 1024),
    )(cells, bias, key_side, value_side)


def per_device(
    latents, row_valid, norm_gain, conv_weight, attn_gain, w_query, w_key, w_value, w_out, cotangent
):
    bf16 = jnp.bfloat16
    shape_all = latents.shape
    rows_dev, col_count, channels = shape_all[1:]
    slab_size = rows_dev * col_count
    frames, slabs = lax.axis_size("tm"), lax.axis_size("rows")
    t = lax.axis_index("tm")
    grad_scale = 1.0 / math.sqrt(frames * slabs * slab_size)

    own_rows = conv_weight.shape[0]
    tap_total = own_rows * frames // channels
    tap_count = max(
        -(-((i * own_rows) % channels + own_rows) // channels) for i in range(frames)
    )
    first_tap = lax.div(t * own_rows, channels)
    weight_from = t * own_rows - first_tap * channels
    own_weight = lax.dynamic_update_slice(
        jnp.zeros((tap_count * channels, channels), bf16), conv_weight, (weight_from, 0)
    )
    k = jnp.minimum(first_tap + jnp.arange(tap_count, dtype=jnp.int32), tap_total - 1)
    taps = jnp.stack([k // 9, k % 9 // 3, k % 3], axis=1)

    cell_factor = jnp.repeat(row_valid.astype(jnp.float32), col_count)[:, None]
    live_cells = cell_factor > 0
    inputs = latents.reshape(slab_size, channels).astype(jnp.float32)
    first_scale = lax.rsqrt(jnp.mean(inputs * inputs, axis=1, keepdims=True) + epsilon)
    normed_one = inputs * first_scale
    gated_in = normed_one * norm_gain
    conv_in = (jax.nn.silu(gated_in) * cell_factor).astype(bf16)

    grad_out = jnp.where(live_cells, cotangent.reshape(slab_size, channels), jnp.zeros((), bf16))

    history = gather_slabs(conv_in.reshape(rows_dev, col_count, channels), 0)
    conv_terms, columns = sum_taps(
        column_shifts(history, 2, 0), taps, own_weight, rows_dev, col_count, False
    )
    conv_terms = conv_terms.reshape(frames, slab_size, channels)
    (conv_terms,) = swap_over_tm([conv_terms], 1)
    conv_out = jnp.sum(conv_terms.astype(jnp.float32), axis=0)

    mixed_f = (inputs + conv_out).astype(bf16).astype(jnp.float32)
    second_scale = lax.rsqrt(jnp.mean(mixed_f * mixed_f, axis=1, keepdims=True) + epsilon)
    normed_two = mixed_f * second_scale
    attn_in = (normed_two * attn_gain).astype(bf16)

    flag_rows = jnp.pad(row_valid.astype(bf16), (0, FLAG_ROWS - rows_dev))
    flag_rows = jnp.broadcast_to(flag_rows[:, None], (FLAG_ROWS, channels))
    block_size = slab_size + FLAG_ROWS
    gathered = gather_rows(jnp.concatenate([attn_in, flag_rows], axis=0), 2)
    flags_all = jnp.repeat(gathered[:, slab_size : slab_size + rows_dev, 0], col_count, axis=1)
    flags_all = jnp.pad(flags_all, ((0, 0), (0, FLAG_ROWS)))[:, None, :]
    bias = jnp.where(flags_all > 0, 0.0, -jnp.inf).astype(jnp.float32)

    queries = dot(attn_in, w_query).astype(bf16)
    key_side = contract_last(queries, w_key).astype(bf16)
    d_attended = contract_last(grad_out, w_out).astype(bf16)
    value_side = contract_last(d_attended, w_value).astype(bf16)

    weighted_b, d_cells, key_terms = attention(gathered, bias, key_side, value_side)
    attended = dot(weighted_b, w_value).astype(bf16)
    d_query = dot(d_cells, w_key).astype(bf16)
    grad_stack = (
        jnp.concatenate(
            [
                contract_first(attn_in, d_query),
                contract_first(d_cells, queries),
                contract_first(weighted_b, d_attended),
                contract_first(attended, grad_out),
            ],
            axis=0,
        )
        * grad_scale
    ).astype(bf16)
    stack_rows = grad_stack.shape[0] // (frames * slabs)
    grad_stack = (
        grad_stack.reshape(frames, slabs, stack_rows, channels)
        .transpose(1, 0, 2, 3)
        .reshape(slabs * frames * stack_rows, channels)
    )
    stack_terms = lax.psum_scatter(grad_stack, "rows", scatter_dimension=0, tiled=True)
    (d_attn_in,) = sum_over_rows([key_terms], 3)
    d_normed = contract_last(d_query, w_query) + d_attn_in[:slab_size]
    scaled_two = attn_gain * d_normed
    d_mixed = grad_out.astype(jnp.float32) + second_scale * (
        scaled_two - normed_two * jnp.mean(scaled_two * normed_two, axis=1, keepdims=True)
    )
    d_conv = d_mixed.astype(bf16)

    spread = gather_slabs(d_conv.reshape(rows_dev, col_count, channels), 4)
    spare = columns.shape[0] // (frames * rows_dev) - col_count
    d_conv_all = jnp.pad(spread[:, 1 : 1 + rows_dev], ((0, 0), (0, 0), (0, spare), (0, 0)))
    weight_terms = contract_first(columns, d_conv_all.reshape(-1, channels)) * grad_scale
    weight_terms = lax.dynamic_slice(
        weight_terms.astype(bf16), (weight_from, 0), (own_rows, channels)
    )
    block_rows = own_rows // slabs
    padded_rows = -(-block_rows // 16) * 16
    weight_terms = jnp.pad(
        weight_terms.reshape(slabs, block_rows, channels),
        ((0, 0), (0, padded_rows - block_rows), (0, 0)),
    )
    weight_sums = lax.psum_scatter(
        weight_terms.reshape(slabs * padded_rows, channels), "rows", scatter_dimension=0, tiled=True
    )
    conv_weight_grad = weight_sums[:block_rows].astype(jnp.float32)

    input_terms = sum_taps(
        column_shifts(spread, 0, 2), 2 - taps, own_weight, rows_dev, col_count, True
    )
    input_terms, stack_terms = swap_over_tm(
        [
            input_terms.reshape(frames, slab_size, channels),
            stack_terms.reshape(frames, stack_rows, channels),
        ],
        5,
    )
    attn_weight_grad = jnp.sum(stack_terms.astype(jnp.float32), axis=0)

    d_input = jnp.sum(input_terms.astype(jnp.float32), axis=0) * cell_factor
    scaled_one = norm_gain * d_input * silu_slope(gated_in)
    input_grad = d_mixed + first_scale * (
        scaled_one - normed_one * jnp.mean(scaled_one * normed_one, axis=1, keepdims=True)
    )
    return (input_grad.astype(bf16).reshape(shape_all), conv_weight_grad, attn_weight_grad)


def solution(mesh):
    return jax.shard_map(
        per_device,
        mesh=mesh,
        in_specs=(
            P("tm", "rows", None, None),
            P("rows"),
            P(),
            P("tm", None),
            P(),
            P(),
            P(),
            P(),
            P(),
            P("tm", "rows", None, None),
        ),
        out_specs=(P("tm", "rows", None, None), P(("tm", "rows"), None), P(("tm", "rows"), None)),
        check_vma=False,
    )
```
